32 devices in a mesh: dp: 4 (over y, x), seq: 2 (over core), tensor: 4 (over z).
Axes of the slice: x: 2, y: 2, z: 4, core: 2. Of those that a mesh axis runs over, the one named last changes fastest.
Arguments:
- block_input: bfloat16 [8, 256, 1024], P('dp', 'seq'), may hold values from -6 to 6
- cotangent: bfloat16 [8, 256, 1024], P('dp', 'seq'), may hold values from -6 to 6
- segments: int32 [8, 256], P('dp', 'seq'), may hold values from 0 to 3, as said below
- positions: int32 [8, 256], P('dp', 'seq'), may hold values from 0 to 255, as said below
- w_qkv: bfloat16 [3, 1024, 1024], P(None, ('dp', 'seq'), 'tensor')
- qkv_bias: float32 [3, 1024], P(None, 'tensor'), may hold values from -3 to 3
- w_out: bfloat16 [1024, 1024], P('tensor', ('dp', 'seq')), may hold values from -1.5 to 1.5
- w_fc1: bfloat16 [1024, 4096], P(('dp', 'seq'), 'tensor'), may hold values from -0.1875 to 0.1875
- fc1_bias: float32 [4096], P('tensor'), may hold values from -3 to 3
- w_fc2: bfloat16 [4096, 1024], P('tensor', ('dp', 'seq')), may hold values from -0.09375 to 0.09375
- ln_gains: float32 [2, 1024], replicated, may hold values from 0.5 to 1.5
- row_biases: float32 [4, 1024], replicated, may hold values from -3 to 3
Outputs:
- output: bfloat16 [8, 256, 1024], P('dp', 'seq')
- grad_input: float32 [8, 256, 1024], P('dp', 'seq')
- grad_w_qkv: float32 [3, 1024, 1024], P(None, ('dp', 'seq'), 'tensor')
- grad_w_out: float32 [1024, 1024], P('tensor', ('dp', 'seq'))
- grad_w_fc1: float32 [1024, 4096], P(('dp', 'seq'), 'tensor')
- grad_w_fc2: float32 [4096, 1024], P('tensor', ('dp', 'seq'))
- grad_qkv_bias: float32 [3, 1024], P(None, 'tensor')
- grad_fc1_bias: float32 [4096], P('tensor')
- grad_ln_gains: float32 [2, 1024], replicated
- grad_row_biases: float32 [4, 1024], replicated
The draws below stay inside these ranges and needn't reach their ends.
Inputs may be any that keep to these rules, and one draw needn't show every extreme that they name: `segments`: segment numbers start at 0 and never fall along a sequence; a rise marks the start of a document; the first sequence is one document and the second reaches document number 3. `positions`: each token's position counts the tokens before it in its own document.
All inputs are finite; a program needn't handle non-finite values.
Results may differ from the reference program's by a relative error of at most 0.02.
Values may be sent and summed in bfloat16 or wider, within the bound.
A program may use at most 128 MiB of HBM per device.

```python
import jax
import jax.numpy as jnp
from jax import lax

D = 1024
H = 16
HD = 64
ROT = 16
FF = 4096
SEQS = 8
LENGTH = 256


def layout_draw(key):
    base = jax.random.fold_in(key, 7301)
    cut_key, pick_key = jax.random.split(base)
    cuts = jax.random.randint(cut_key, (SEQS, 3), 1, LENGTH)
    active = jax.random.randint(pick_key, (SEQS, 3), 0, 2)
    row_ids = jnp.arange(SEQS)[:, None]
    active = jnp.where(row_ids == 0, 0, jnp.where(row_ids == 1, 1, active))
    token_ids = jnp.arange(LENGTH)
    passed = active[:, None, :] * (token_ids[None, :, None] >= cuts[:, None, :]).astype(jnp.int32)
    seg_ids = jnp.sum(passed, axis=-1)
    starts = jnp.max(passed * cuts[:, None, :], axis=-1)
    return (seg_ids.astype(jnp.int32), (token_ids[None, :] - starts).astype(jnp.int32))


def draw_segments(key, part):
    return layout_draw(key)[0]


def draw_positions(key, part):
    return layout_draw(key)[1]


def draw_w_qkv(key, part):
    normal_key = jax.random.fold_in(jax.random.fold_in(key, 4409), 0)
    base = jax.random.normal(normal_key, (3, D, D), jnp.float32) * D ** (-0.5)
    return base.astype(jnp.bfloat16)


def shard_levels(stream_key, shape, cuts, least, top_value):
    def one(dim, parts):
        steps = jax.random.uniform(jax.random.fold_in(jax.random.fold_in(stream_key, 6), dim), (parts,), jnp.float32, least / len(cuts), top_value / len(cuts))
        return jnp.repeat(jnp.exp(steps), shape[dim] // parts).reshape((-1,) + (1,) * (len(shape) - dim - 1))

    factor_of = one(*cuts[0])
    for cut in cuts[1:]:
        factor_of = factor_of * one(*cut)
    return factor_of


def gaussian(stream_key, dims, scale, limit, cuts=(), held_as=jnp.bfloat16):
    entries = jax.random.normal(stream_key, dims, jnp.float32) * scale
    if len(cuts) > 0:
        entries = shard_levels(stream_key, dims, cuts, -0.22, 0.18) * entries
    return jnp.clip(entries, min=-limit, max=limit).astype(held_as)


def setup_inputs(seed: int = 0) -> dict:
    keys = jax.random.split(jax.random.key(seed), 13)
    block_input = gaussian(keys[0], (SEQS, LENGTH, D), 1.0, 6.0, ((0, 4), (1, 2)))
    cotangent = gaussian(keys[1], (SEQS, LENGTH, D), 1.0, 6.0, ((0, 4), (1, 2)))
    segments = draw_segments(jax.random.fold_in(keys[12], 71), 0)
    positions = draw_positions(jax.random.fold_in(keys[12], 71), 0)
    w_qkv = draw_w_qkv(jax.random.fold_in(keys[12], 71), 0)
    qkv_bias = gaussian(keys[5], (3, D), 0.5, 3.0, ((1, 4),), jnp.float32)
    w_out = gaussian(keys[6], (D, D), (D // 64) ** -0.5, 1.5, ((0, 4), (1, 8)))
    w_fc1 = gaussian(keys[7], (D, FF), D ** -0.5, 0.1875, ((0, 8), (1, 4)))
    fc1_bias = gaussian(keys[8], (FF,), 0.5, 3.0, ((0, 4),), jnp.float32)
    w_fc2 = gaussian(keys[9], (FF, D), FF ** -0.5, 0.09375, ((0, 4), (1, 8)))
    ln_gains = jnp.clip(1.0 + 0.1 * jax.random.normal(keys[10], (2, D), jnp.float32), 0.5, 1.5)
    row_biases = gaussian(keys[11], (4, D), 0.5, 3.0, (), jnp.float32)
    return dict(block_input=block_input, cotangent=cotangent, segments=segments, positions=positions, w_qkv=w_qkv, qkv_bias=qkv_bias, w_out=w_out, w_fc1=w_fc1, fc1_bias=fc1_bias, w_fc2=w_fc2, ln_gains=ln_gains, row_biases=row_biases)


norm_eps = 1e-05
neg_big = -1e+30
inv_root_two = 0.7071067811865476
inv_root_tau = 0.3989422804014327

def rounded(values):
    return lax.optimization_barrier(values.astype(jnp.bfloat16))

def layer_norm(values, gain, shift):
    centred = values - lax.optimization_barrier(jnp.mean(values, axis=-1, keepdims=True))
    inv_std = lax.rsqrt(lax.optimization_barrier(jnp.mean(centred * centred, axis=-1, keepdims=True)) + norm_eps)
    normed = centred * inv_std
    return (normed * gain + shift, normed, inv_std)

def norm_back(grad_out, normed, inv_std, gain):
    scaled = grad_out * gain
    centre = lax.optimization_barrier(jnp.mean(scaled, axis=-1, keepdims=True))
    slope = lax.optimization_barrier(jnp.mean(scaled * normed, axis=-1, keepdims=True))
    return inv_std * (scaled - centre - normed * slope)

def gelu_pair(pre_act):
    cumul = 0.5 * (1.0 + lax.erf(pre_act * inv_root_two))
    return (pre_act * cumul, cumul + pre_act * inv_root_tau * jnp.exp(-0.5 * pre_act * pre_act))

def rotary_tables(positions):
    half_rot = ROT // 2
    freqs = 10000.0 ** (-2.0 * jnp.arange(half_rot).astype(jnp.float32) / ROT)
    angles = positions.astype(jnp.float32)[..., None] * freqs
    cosine = jnp.cos(angles)
    sine = jnp.sin(angles)
    return (jnp.concatenate([cosine, cosine], -1)[..., None, :], jnp.concatenate([sine, sine], -1)[..., None, :])

def rotate(tensor, cosine, sine):
    half_rot = ROT // 2
    head = tensor[..., :ROT]
    turned = jnp.concatenate([-head[..., half_rot:], head[..., :half_rot]], -1)
    return jnp.concatenate([head * cosine + turned * sine, tensor[..., ROT:]], -1)

def unrotate(grads, cosine, sine):
    half_rot = ROT // 2
    head = grads[..., :ROT]
    times_sine = head * sine
    back = jnp.concatenate([times_sine[..., half_rot:], -times_sine[..., :half_rot]], -1)
    return jnp.concatenate([head * cosine + back, grads[..., ROT:]], -1)

def reference(block_input, cotangent, segments, positions, w_qkv, qkv_bias, w_out, w_fc1, fc1_bias, w_fc2, ln_gains, row_biases):
    qkv_float = w_qkv.astype(jnp.float32)
    scale = HD ** (-0.5)
    token_ids = jnp.arange(LENGTH)
    causal = token_ids[None, :] <= token_ids[:, None]

    def one_sequence(totals, inputs):
        tokens, grad_y, seg_ids, seq_pos = inputs
        tokens_f = tokens.astype(jnp.float32)
        first_out, first_normed, first_inv = layer_norm(tokens_f, ln_gains[0], row_biases[0])
        second_out, second_normed, second_inv = layer_norm(tokens_f, ln_gains[1], row_biases[1])
        first_norm_input = rounded(first_out)
        second_norm_input = rounded(second_out)
        projected = jnp.einsum('ld,jdc->jlc', first_norm_input.astype(jnp.float32), qkv_float) + qkv_bias[:, None, :]
        cosine, sine = rotary_tables(seq_pos)
        queries = rounded(rotate(projected[0].reshape(LENGTH, H, HD), cosine, sine))
        keys_rot = rounded(rotate(projected[1].reshape(LENGTH, H, HD), cosine, sine))
        values_in = rounded(projected[2].reshape(LENGTH, H, HD))
        queries_f = queries.astype(jnp.float32)
        keys_f = keys_rot.astype(jnp.float32)
        values_f = values_in.astype(jnp.float32)
        scores = jnp.einsum('qhd,khd->hqk', queries_f, keys_f) * scale
        allowed = ((seg_ids[:, None] == seg_ids[None, :]) & causal)[None]
        row_max = lax.optimization_barrier(jnp.max(jnp.where(allowed, scores, neg_big), axis=-1, keepdims=True))
        expo = jnp.where(allowed, jnp.exp(scores - row_max), 0.0)
        row_sum = lax.optimization_barrier(jnp.sum(expo, axis=-1, keepdims=True))
        log_sum = row_max + jnp.log(row_sum)
        mixed = jnp.einsum('hqk,khd->hqd', rounded(expo).astype(jnp.float32), values_f) / row_sum
        attention_context = rounded(mixed.transpose(1, 0, 2).reshape(LENGTH, D))
        attn_out = jnp.dot(attention_context, w_out, preferred_element_type=jnp.float32)
        pre_act = jnp.dot(second_norm_input, w_fc1, preferred_element_type=jnp.float32) + fc1_bias
        activ, gelu_slope = gelu_pair(pre_act)
        hidden_activation = rounded(activ)
        mlp_out = jnp.dot(hidden_activation, w_fc2, preferred_element_type=jnp.float32)
        output = (tokens_f + attn_out + row_biases[2] + mlp_out + row_biases[3]).astype(jnp.bfloat16)
        grad_f = grad_y.astype(jnp.float32)
        gradient_output_weight = jnp.dot(attention_context.T, grad_y, preferred_element_type=jnp.float32)
        grad_context = rounded(jnp.dot(grad_y, w_out.T, preferred_element_type=jnp.float32))
        gradient_down_weight = jnp.dot(hidden_activation.T, grad_y, preferred_element_type=jnp.float32)
        grad_pre = jnp.dot(grad_y, w_fc2.T, preferred_element_type=jnp.float32) * gelu_slope
        gradient_hidden_input = rounded(grad_pre)
        grad_fc1_w = jnp.dot(second_norm_input.T, gradient_hidden_input, preferred_element_type=jnp.float32)
        grad_second = jnp.dot(gradient_hidden_input, w_fc1.T, preferred_element_type=jnp.float32)
        grad_ctx3 = grad_context.reshape(LENGTH, H, HD).astype(jnp.float32)
        delta = lax.optimization_barrier(jnp.sum(grad_ctx3 * attention_context.reshape(LENGTH, H, HD).astype(jnp.float32), axis=-1)).T
        probs = jnp.where(allowed, jnp.exp(scores - log_sum), 0.0)
        grad_values = jnp.einsum('hqk,qhd->khd', rounded(probs).astype(jnp.float32), grad_ctx3)
        grad_probs = jnp.einsum('qhd,khd->hqk', grad_ctx3, values_f)
        grad_scores = rounded(probs * (grad_probs - delta[:, :, None])).astype(jnp.float32)
        grad_queries = jnp.einsum('hqk,khd->qhd', grad_scores, keys_f) * scale
        grad_keys = jnp.einsum('hqk,qhd->khd', grad_scores, queries_f) * scale
        grad_proj = jnp.stack([unrotate(grad_queries, cosine, sine).reshape(LENGTH, D), unrotate(grad_keys, cosine, sine).reshape(LENGTH, D), grad_values.reshape(LENGTH, D)])
        gradient_projection_input = rounded(grad_proj).astype(jnp.float32)
        grad_qkv_w = jnp.einsum('ld,jlc->jdc', first_norm_input.astype(jnp.float32), gradient_projection_input)
        grad_first = jnp.einsum('jlc,jdc->ld', gradient_projection_input, qkv_float)
        grad_tokens = grad_f + norm_back(grad_first, first_normed, first_inv, ln_gains[0]) + norm_back(grad_second, second_normed, second_inv, ln_gains[1])
        grad_gain_pair = jnp.stack([lax.optimization_barrier(jnp.sum(grad_first * first_normed, axis=0)), lax.optimization_barrier(jnp.sum(grad_second * second_normed, axis=0))])
        grad_rows = jnp.stack([lax.optimization_barrier(jnp.sum(grad_first, axis=0)), lax.optimization_barrier(jnp.sum(grad_second, axis=0)), lax.optimization_barrier(jnp.sum(grad_f, axis=0)), lax.optimization_barrier(jnp.sum(grad_f, axis=0))])
        updated = (totals[0] + grad_qkv_w, totals[1] + gradient_output_weight, totals[2] + grad_fc1_w, totals[3] + gradient_down_weight, totals[4] + lax.optimization_barrier(jnp.sum(grad_proj, axis=1)), totals[5] + lax.optimization_barrier(jnp.sum(grad_pre, axis=0)), totals[6] + grad_gain_pair, totals[7] + grad_rows)
        return (updated, (output, grad_tokens))
    start_totals = (jnp.zeros((3, D, D), jnp.float32), jnp.zeros((D, D), jnp.float32), jnp.zeros((D, FF), jnp.float32), jnp.zeros((FF, D), jnp.float32), jnp.zeros((3, D), jnp.float32), jnp.zeros((FF,), jnp.float32), jnp.zeros((2, D), jnp.float32), jnp.zeros((4, D), jnp.float32))
    totals, results = lax.scan(one_sequence, start_totals, (block_input, cotangent, segments, positions))
    return (results[0], results[1], totals[0], totals[1], totals[2], totals[3], totals[4], totals[5], totals[6], totals[7])
```

```python
import functools
import math

import jax
import jax.numpy as jnp
from jax import lax
from jax.experimental import pallas as pl
from jax.experimental.pallas import tpu as pltpu
from jax.sharding import PartitionSpec as P

HD = 64
ROT = 16


norm_eps = 1e-05
neg_big = -1e30
inv_root_two = 0.7071067811865476
inv_root_tau = 0.3989422804014327


def layer_norm(values, gain, shift):
    centred = values - jnp.mean(values, axis=-1, keepdims=True)
    inv_std = lax.rsqrt(jnp.mean(centred * centred, axis=-1, keepdims=True) + norm_eps)
    normed = centred * inv_std
    return (normed * gain + shift, normed, inv_std)


def norm_back(grad_out, normed, inv_std, gain):
    scaled = grad_out * gain
    centre = jnp.mean(scaled, axis=-1, keepdims=True)
    slope = jnp.mean(scaled * normed, axis=-1, keepdims=True)
    return inv_std * (scaled - centre - normed * slope)


def gelu_pair(pre_act):
    cumul = 0.5 * (1.0 + lax.erf(pre_act * inv_root_two))
    return (pre_act * cumul, cumul + pre_act * inv_root_tau * jnp.exp(-0.5 * pre_act * pre_act))


def rotary_tables(positions):
    half_rot = ROT // 2
    freqs = 10000.0 ** (-2.0 * jnp.arange(half_rot).astype(jnp.float32) / ROT)
    angles = positions.astype(jnp.float32)[..., None] * freqs
    cosine = jnp.cos(angles)
    sine = jnp.sin(angles)
    return (
        jnp.concatenate([cosine, cosine], -1)[..., None, :],
        jnp.concatenate([sine, sine], -1)[..., None, :],
    )


def rotate(tensor, cosine, sine):
    half_rot = ROT // 2
    head = tensor[..., :ROT]
    turned = jnp.concatenate([-head[..., half_rot:], head[..., :half_rot]], -1)
    return jnp.concatenate([head * cosine + turned * sine, tensor[..., ROT:]], -1)


def unrotate(grads, cosine, sine):
    half_rot = ROT // 2
    head = grads[..., :ROT]
    times_sine = head * sine
    back = jnp.concatenate([times_sine[..., half_rot:], -times_sine[..., :half_rot]], -1)
    return jnp.concatenate([head * cosine + back, grads[..., ROT:]], -1)


def gather_keys(keys_flat, values_in, segments):
    return (
        lax.all_gather(keys_flat, "seq", axis=1, tiled=True),
        lax.all_gather(values_in, "seq", axis=1, tiled=True),
        lax.all_gather(segments, "seq", axis=1, tiled=True),
    )


def pair_terms(
    query_blk,
    query_pos,
    query_seg,
    key_blk,
    value_blk,
    key_pos,
    key_seg,
    grad_blk,
    log_blk,
    delta_blk,
    scale,
):
    scores = (
        jnp.einsum("sqhd,skhd->shqk", query_blk, key_blk, preferred_element_type=jnp.float32)
        * scale
    )
    same_doc = query_seg[:, None, :, None] == key_seg[:, None, None, :]
    earlier = key_pos[None, None, None, :] <= query_pos[None, None, :, None]
    probs = jnp.where(same_doc & earlier, jnp.exp(scores - log_blk[..., None]), 0.0)
    grad_p = jnp.einsum("sqhd,skhd->shqk", grad_blk, value_blk, preferred_element_type=jnp.float32)
    grad_s = (probs * (grad_p - delta_blk[..., None])).astype(jnp.bfloat16)
    return (probs, grad_s)


def shards(
    block_input,
    cotangent,
    segments,
    positions,
    w_qkv,
    qkv_bias,
    w_out,
    w_fc1,
    fc1_bias,
    w_fc2,
    ln_gains,
    row_biases,
):
    seqs_here, rows_here, width = block_input.shape
    heads_here = w_qkv.shape[2] // HD
    flat_width = heads_here * HD
    scale = HD ** (-0.5)
    shape_heads = (seqs_here, rows_here, heads_here, HD)
    forward_weights = (
        lax.all_gather(w_qkv, ("dp", "seq"), axis=1, tiled=True),
        lax.all_gather(w_out, ("dp", "seq"), axis=1, tiled=True),
        lax.all_gather(w_fc1, ("dp", "seq"), axis=0, tiled=True),
        lax.all_gather(w_fc2, ("dp", "seq"), axis=1, tiled=True),
    )
    query_key_value_gathered, output_weight_gathered, up_weight_gathered, down_weight_gathered = (
        forward_weights
    )
    inputs_f = block_input.astype(jnp.float32)
    first_out, first_normed, first_inv = layer_norm(inputs_f, ln_gains[0], row_biases[0])
    second_out, second_normed, second_inv = layer_norm(inputs_f, ln_gains[1], row_biases[1])
    first_norm_input = first_out.astype(jnp.bfloat16)
    second_norm_input = second_out.astype(jnp.bfloat16)
    projected = (
        jnp.einsum(
            "bxf,kfh->kbxh",
            first_norm_input,
            query_key_value_gathered,
            preferred_element_type=jnp.float32,
        )
        + qkv_bias[:, None, None, :]
    )
    cosine, sine = rotary_tables(positions)
    queries = rotate(projected[0].reshape(shape_heads), cosine, sine).astype(jnp.bfloat16)
    keys_flat = (
        rotate(projected[1].reshape(shape_heads), cosine, sine)
        .astype(jnp.bfloat16)
        .reshape(seqs_here, rows_here, flat_width)
    )
    values_in = projected[2].astype(jnp.bfloat16)
    query_pos = lax.axis_index("seq") * rows_here + jnp.arange(rows_here)

    def block_scores(key_block, seg_block, key_start):
        count = key_block.shape[1]
        keys_heads = key_block.reshape(seqs_here, count, heads_here, HD)
        scores = (
            jnp.einsum("sqhd,skhd->shqk", queries, keys_heads, preferred_element_type=jnp.float32)
            * scale
        )
        key_pos = key_start + jnp.arange(count)
        same_doc = segments[:, None, :, None] == seg_block[:, None, None, :]
        earlier = key_pos[None, None, None, :] <= query_pos[None, None, :, None]
        return (scores, same_doc & earlier)

    start_state = (
        jnp.full((seqs_here, heads_here, rows_here), neg_big, jnp.float32),
        jnp.zeros((seqs_here, heads_here, rows_here), jnp.float32),
        jnp.zeros((seqs_here, heads_here, rows_here, HD), jnp.float32),
    )
    key_part = lax.all_gather(keys_flat, "seq", axis=1, tiled=True)
    value_part = lax.all_gather(values_in, "seq", axis=1, tiled=True)
    seg_part = lax.all_gather(segments, "seq", axis=1, tiled=True)
    count = key_part.shape[1]
    attend_block = math.gcd(count, 512)

    def step_block(block_idx, state):
        run_max, run_sum, accum = state
        offset = block_idx * attend_block
        key_block = lax.dynamic_slice_in_dim(key_part, offset, attend_block, 1)
        value_block = lax.dynamic_slice_in_dim(value_part, offset, attend_block, 1).reshape(
            seqs_here, attend_block, heads_here, HD
        )
        seg_block = lax.dynamic_slice_in_dim(seg_part, offset, attend_block, 1)
        scores, allowed = block_scores(key_block, seg_block, offset)
        new_max = jnp.maximum(run_max, jnp.max(jnp.where(allowed, scores, neg_big), axis=-1))
        factor = jnp.exp(run_max - new_max)
        expo = jnp.where(allowed, jnp.exp(scores - new_max[..., None]), 0.0)
        new_sum = run_sum * factor + jnp.sum(expo, axis=-1)
        update = jnp.einsum(
            "shqk,skhd->shqd",
            expo.astype(jnp.bfloat16),
            value_block,
            preferred_element_type=jnp.float32,
        )
        return (new_max, new_sum, accum * factor[..., None] + update)

    run_max, run_sum, accum = lax.fori_loop(0, count // attend_block, step_block, start_state)
    log_sum = run_max + jnp.log(run_sum)
    attention_context = (
        (accum / run_sum[..., None])
        .transpose(0, 2, 1, 3)
        .reshape(seqs_here, rows_here, flat_width)
        .astype(jnp.bfloat16)
    )
    pre_act = (
        jnp.einsum(
            "vrk,kt->vrt", second_norm_input, up_weight_gathered, preferred_element_type=jnp.float32
        )
        + fc1_bias
    )
    activ, gelu_slope = gelu_pair(pre_act)
    hidden_activation = activ.astype(jnp.bfloat16)
    partial_output_sum = jnp.einsum(
        "qhw,wj->qhj", attention_context, output_weight_gathered, preferred_element_type=jnp.float32
    )
    partial_output_sum = partial_output_sum + jnp.einsum(
        "qzg,gc->qzc", hidden_activation, down_weight_gathered, preferred_element_type=jnp.float32
    )
    branches = lax.psum(partial_output_sum.astype(jnp.bfloat16), "tensor").astype(jnp.float32)
    output = (inputs_f + branches + row_biases[2] + row_biases[3]).astype(jnp.bfloat16)
    query_key_value_backward, output_weight_backward, up_weight_backward, down_weight_backward = (
        lax.all_gather(w_qkv, ("dp", "seq"), axis=1, tiled=True),
        lax.all_gather(w_out, ("dp", "seq"), axis=1, tiled=True),
        lax.all_gather(w_fc1, ("dp", "seq"), axis=0, tiled=True),
        lax.all_gather(w_fc2, ("dp", "seq"), axis=1, tiled=True),
    )
    grad_f = cotangent.astype(jnp.float32)
    gradient_output_weight = jnp.einsum(
        "bxz,bxe->ze", attention_context, cotangent, preferred_element_type=jnp.float32
    )
    grad_context = jnp.einsum(
        "zpi,xi->zpx", cotangent, output_weight_backward, preferred_element_type=jnp.float32
    ).astype(jnp.bfloat16)
    gradient_down_weight = jnp.einsum(
        "tzi,tzo->io", hidden_activation, cotangent, preferred_element_type=jnp.float32
    )
    grad_pre = (
        jnp.einsum(
            "hvg,rg->hvr", cotangent, down_weight_backward, preferred_element_type=jnp.float32
        )
        * gelu_slope
    )
    gradient_hidden_input = grad_pre.astype(jnp.bfloat16)
    grad_fc1_w = jnp.einsum(
        "mxa,mxr->ar", second_norm_input, gradient_hidden_input, preferred_element_type=jnp.float32
    )
    grad_second = jnp.einsum(
        "ikq,uq->iku", gradient_hidden_input, up_weight_backward, preferred_element_type=jnp.float32
    )
    grad_ctx_heads = grad_context.reshape(shape_heads)
    delta = jnp.sum(
        grad_ctx_heads.astype(jnp.float32)
        * attention_context.reshape(shape_heads).astype(jnp.float32),
        axis=-1,
    ).transpose(0, 2, 1)
    key_all, value_all, seg_all = gather_keys(keys_flat, values_in, segments)
    total_len = key_all.shape[1]
    block = math.gcd(total_len, 512)

    def key_slices(offset):
        key_block = lax.dynamic_slice_in_dim(key_all, offset, block, 1).reshape(
            seqs_here, block, heads_here, HD
        )
        value_block = lax.dynamic_slice_in_dim(value_all, offset, block, 1).reshape(
            seqs_here, block, heads_here, HD
        )
        seg_block = lax.dynamic_slice_in_dim(seg_all, offset, block, 1)
        return (key_block, value_block, seg_block)

    def back_block(block_idx, state):
        grad_q, grad_key_all, grad_value_all = state
        offset = block_idx * block
        key_block, value_block, seg_block = key_slices(offset)
        probs, grad_s = pair_terms(
            queries,
            query_pos,
            segments,
            key_block,
            value_block,
            offset + jnp.arange(block),
            seg_block,
            grad_ctx_heads,
            log_sum,
            delta,
            scale,
        )
        grad_v = jnp.einsum(
            "shqk,sqhd->skhd",
            probs.astype(jnp.bfloat16),
            grad_ctx_heads,
            preferred_element_type=jnp.float32,
        )
        grad_q = (
            grad_q
            + jnp.einsum("shqk,skhd->sqhd", grad_s, key_block, preferred_element_type=jnp.float32)
            * scale
        )
        grad_k = (
            jnp.einsum("shqk,sqhd->skhd", grad_s, queries, preferred_element_type=jnp.float32)
            * scale
        )
        grad_key_all = lax.dynamic_update_slice_in_dim(
            grad_key_all, grad_k.reshape(seqs_here, block, flat_width), offset, 1
        )
        grad_value_all = lax.dynamic_update_slice_in_dim(
            grad_value_all, grad_v.reshape(seqs_here, block, flat_width), offset, 1
        )
        return (grad_q, grad_key_all, grad_value_all)

    back_start = (
        jnp.zeros(shape_heads, jnp.float32),
        jnp.zeros((seqs_here, total_len, flat_width), jnp.float32),
        jnp.zeros((seqs_here, total_len, flat_width), jnp.float32),
    )
    grad_q, grad_key_all, grad_value_all = lax.fori_loop(
        0, total_len // block, back_block, back_start
    )
    grad_key_here, grad_value_here = (
        lax.psum_scatter(
            grad_key_all.astype(jnp.bfloat16), "seq", scatter_dimension=1, tiled=True
        ).astype(jnp.float32),
        lax.psum_scatter(
            grad_value_all.astype(jnp.bfloat16), "seq", scatter_dimension=1, tiled=True
        ).astype(jnp.float32),
    )
    grad_proj = jnp.stack(
        [
            unrotate(grad_q, cosine, sine).reshape(seqs_here, rows_here, flat_width),
            unrotate(grad_key_here.reshape(shape_heads), cosine, sine).reshape(
                seqs_here, rows_here, flat_width
            ),
            grad_value_here,
        ]
    )
    grad_bias_qkv = jnp.sum(grad_proj, axis=(1, 2))
    gradient_projection_input = grad_proj.astype(jnp.bfloat16)
    grad_qkv_w = jnp.einsum(
        "ink,oint->okt",
        first_norm_input,
        gradient_projection_input,
        preferred_element_type=jnp.float32,
    )
    grad_first = jnp.einsum(
        "etbp,eop->tbo",
        gradient_projection_input,
        query_key_value_backward,
        preferred_element_type=jnp.float32,
    )
    grad_first, grad_second = (
        lax.psum(grad_first.astype(jnp.bfloat16), "tensor").astype(jnp.float32),
        lax.psum(grad_second.astype(jnp.bfloat16), "tensor").astype(jnp.float32),
    )
    grad_input = (
        grad_f
        + norm_back(grad_first, first_normed, first_inv, ln_gains[0])
        + norm_back(grad_second, second_normed, second_inv, ln_gains[1])
    )
    gain_terms = jnp.stack(
        [
            jnp.sum(grad_first * first_normed, axis=(0, 1)),
            jnp.sum(grad_second * second_normed, axis=(0, 1)),
        ]
    )
    row_terms = jnp.stack(
        [
            jnp.sum(grad_first, axis=(0, 1)),
            jnp.sum(grad_second, axis=(0, 1)),
            jnp.sum(grad_f, axis=(0, 1)),
            jnp.sum(grad_f, axis=(0, 1)),
        ]
    )
    bias_sums = lax.psum(
        (grad_bias_qkv, jnp.sum(grad_pre, axis=(0, 1)), gain_terms, row_terms), ("dp", "seq")
    )
    weight_sums = (
        lax.psum_scatter(grad_qkv_w, ("dp", "seq"), scatter_dimension=1, tiled=True),
        lax.psum_scatter(gradient_output_weight, ("dp", "seq"), scatter_dimension=1, tiled=True),
        lax.psum_scatter(grad_fc1_w, ("dp", "seq"), scatter_dimension=0, tiled=True),
        lax.psum_scatter(gradient_down_weight, ("dp", "seq"), scatter_dimension=1, tiled=True),
    )
    return (
        output,
        grad_input,
        weight_sums[0],
        weight_sums[1],
        weight_sums[2],
        weight_sums[3],
        bias_sums[0],
        bias_sums[1],
        bias_sums[2],
        bias_sums[3],
    )


MESH = pl.DeviceIdType.MESH
ANY = pl.BlockSpec(memory_space=pl.ANY)
VM = pl.BlockSpec(memory_space=pltpu.VMEM)


def shard_views(refs, index, sizes):
    spans = [pl.ds(pl.multiple_of(index * n, n), n) for n in sizes]
    return (
        refs[0].at[:, spans[0], :],
        refs[1].at[:, spans[1]],
        refs[2].at[spans[2], :],
        refs[3].at[:, spans[3]],
    )


def remote(src, dst, send, recv, where):
    return pltpu.make_async_remote_copy(
        src_ref=src, dst_ref=dst, send_sem=send, recv_sem=recv, device_id=where, device_id_type=MESH
    )


def gather_kernel(ndp, sizes, *refs):
    (wq, wo, w1, w2, x, c, sp, gq, go, g1, g2, gx, gc, gsp) = refs[:14]
    send, recv, send2, recv2, local, psend, precv, plocal = refs[14:]
    nseq = 2
    d, s = lax.axis_index("dp"), lax.axis_index("seq")
    other = 1 - s
    shards_in = (wq, wo, w1, w2)
    full = (gq, go, g1, g2)
    pairs = ((x, gx), (c, gc), (sp, gsp))

    barrier = pltpu.get_barrier_semaphore()
    for k in range(1, ndp):
        pl.semaphore_signal(barrier, inc=1, device_id={"dp": lax.rem(d + k, ndp)}, device_id_type=MESH)
    pl.semaphore_signal(barrier, inc=1, device_id={"seq": other}, device_id_type=MESH)
    pl.semaphore_wait(barrier, ndp)

    mine = shard_views(full, d * nseq + s, sizes)
    far = []
    near = []
    for a in range(4):
        for k in range(1, ndp):
            copy = remote(
                shards_in[a], mine[a], send.at[a, k], recv.at[a, k], {"dp": lax.rem(d + k, ndp)}
            )
            copy.start()
            far.append((a, k, copy))
    for j, (src, dst) in enumerate(pairs):
        copy = remote(src, dst.at[:, s], psend.at[j], precv.at[j], {"seq": other})
        copy.start()
        near.append(copy)
    here = []
    for j, (src, dst) in enumerate(pairs):
        copy = pltpu.make_async_copy(src, dst.at[:, s], plocal.at[j])
        copy.start()
        here.append(copy)
    for a in range(4):
        copy = remote(shards_in[a], mine[a], send2.at[a, 0], recv2.at[a, 0], {"seq": other})
        copy.start()
        near.append(copy)
        copy = pltpu.make_async_copy(shards_in[a], mine[a], local.at[a])
        copy.start()
        here.append(copy)
    for a, k, copy in far:
        copy.wait_recv()
        view = shard_views(full, lax.rem(d + ndp - k, ndp) * nseq + s, sizes)[a]
        onward = remote(view, view, send2.at[a, k], recv2.at[a, k], {"seq": other})
        onward.start()
        near.append(onward)
    for copy in here:
        copy.wait()
    for _, _, copy in far:
        copy.wait_send()
    for copy in near:
        copy.wait()


def reduce_kernel(ndp, nt, sizes, *refs):
    (pq, po, p1, p2, zin, bin_) = refs[:6]
    (oq, oo, o1, o2, zout, bout) = refs[6:12]
    own = refs[12:16]
    got1 = refs[16:20]
    got2 = refs[20:24]
    zgot, bpair, bsum, bgot2, bsum2, bgot3 = refs[24:30]
    (s1, r1, l1, s2, r2, zs, zr, as_, ar, b1s, b1r, b2s, b2r, b3s, b3r) = refs[30:]
    nseq = 2
    partial = (pq, po, p1, p2)
    outs = (oq, oo, o1, o2)
    d, s, t = lax.axis_index("dp"), lax.axis_index("seq"), lax.axis_index("tensor")
    other = 1 - s
    rows = zin.shape[1] // nt

    barrier = pltpu.get_barrier_semaphore()
    for k in range(1, ndp):
        pl.semaphore_signal(barrier, inc=1, device_id={"dp": lax.rem(d + k, ndp)}, device_id_type=MESH)
    for k in range(1, nt):
        pl.semaphore_signal(
            barrier, inc=1, device_id={"tensor": lax.rem(t + k, nt)}, device_id_type=MESH
        )
    pl.semaphore_signal(barrier, inc=1, device_id={"seq": other}, device_id_type=MESH)
    pl.semaphore_wait(barrier, ndp + nt - 1)

    def band(index):
        return pl.ds(pl.multiple_of(index * rows, rows), rows)

    zsends = []
    for k in range(1, nt):
        peer = lax.rem(t + k, nt)
        copy = remote(zin.at[:, band(peer)], zgot.at[k], zs.at[k], zr.at[k], {"tensor": peer})
        copy.start()
        zsends.append(copy)
    first = {}
    mine = {}
    order = list(range(1, ndp)) + [0]
    for k in order:
        dest = lax.rem(d + k, ndp)
        give = shard_views(partial, dest * nseq + other, sizes)
        keep = shard_views(partial, dest * nseq + s, sizes)
        for a in range(4):
            copy = remote(give[a], got1[a].at[k], s1.at[a, k], r1.at[a, k], {"seq": other})
            copy.start()
            first[a, k] = copy
            copy = pltpu.make_async_copy(keep[a], own[a].at[k], l1.at[a, k])
            copy.start()
            mine[a, k] = copy
    bpair_copy = remote(bin_, bpair, b1s, b1r, {"seq": other})
    bpair_copy.start()

    second = {}
    for k in order:
        for a in range(4):
            mine[a, k].wait()
            first[a, k].wait_recv()
            own[a][k] = (
                own[a][k].astype(jnp.float32) + got1[a][k].astype(jnp.float32)
            ).astype(own[a].dtype)
            if k:
                copy = remote(
                    own[a].at[k], got2[a].at[k], s2.at[a, k], r2.at[a, k], {"dp": lax.rem(d + k, ndp)}
                )
                copy.start()
                second[a, k] = copy

    bpair_copy.wait()
    bsum[...] = bin_[...] + bpair[...]
    bsends = []
    for k in range(1, ndp):
        copy = remote(bsum, bgot2.at[d], b2s.at[k], b2r.at[k], {"dp": lax.rem(d + k, ndp)})
        copy.start()
        bsends.append(copy)

    total = zin[:, band(t)].astype(jnp.float32)
    for k, copy in zip(range(1, nt), zsends):
        copy.wait_recv()
        total = total + zgot[k].astype(jnp.float32)
    zout[:, band(t)] = total.astype(zout.dtype)
    asends = []
    for k in range(1, nt):
        peer = lax.rem(t + k, nt)
        copy = remote(
            zout.at[:, band(t)], zout.at[:, band(t)], as_.at[k], ar.at[k], {"tensor": peer}
        )
        copy.start()
        asends.append(copy)

    for copy in bsends:
        copy.wait()
    bgot2[d] = bsum[...]
    plane = bgot2[0]
    for k in range(1, ndp):
        plane = plane + bgot2[k]
    bsum2[...] = plane
    bsends = []
    for k in range(1, nt):
        copy = remote(bsum2, bgot3.at[t], b3s.at[k], b3r.at[k], {"tensor": lax.rem(t + k, nt)})
        copy.start()
        bsends.append(copy)

    for a in range(4):
        acc = own[a][0].astype(jnp.float32)
        for k in range(1, ndp):
            second[a, k].wait_recv()
            acc = acc + got2[a][k].astype(jnp.float32)
        outs[a][...] = acc

    for copy in bsends:
        copy.wait()
    bgot3[t] = bsum2[...]
    whole = bgot3[0]
    for k in range(1, nt):
        whole = whole + bgot3[k]
    bout[0] = bsum2[...]
    bout[1] = whole
    for copy in asends:
        copy.wait()
    for copy in zsends:
        copy.wait_send()
    for copy in first.values():
        copy.wait_send()
    for copy in second.values():
        copy.wait_send()


def gather_all(ndp, sizes, w_qkv, w_out, w_fc1, w_fc2, tokens, cotangent, ids):
    shape = jax.ShapeDtypeStruct
    many = ndp * 2
    seqs, rows, width = tokens.shape
    dma = pltpu.SemaphoreType.DMA
    return pl.pallas_call(
        functools.partial(gather_kernel, ndp, sizes),
        out_shape=(
            shape((w_qkv.shape[0], w_qkv.shape[1] * many, w_qkv.shape[2]), w_qkv.dtype),
            shape((w_out.shape[0], w_out.shape[1] * many), w_out.dtype),
            shape((w_fc1.shape[0] * many, w_fc1.shape[1]), w_fc1.dtype),
            shape((w_fc2.shape[0], w_fc2.shape[1] * many), w_fc2.dtype),
            shape((seqs, 2, rows, width), tokens.dtype),
            shape((seqs, 2, rows, width), cotangent.dtype),
            shape((ids.shape[0], 2) + ids.shape[1:], ids.dtype),
        ),
        in_specs=[VM] * 7,
        out_specs=[ANY] * 7,
        scratch_shapes=[
            dma((4, ndp)),
            dma((4, ndp)),
            dma((4, ndp)),
            dma((4, ndp)),
            dma((4,)),
            dma((3,)),
            dma((3,)),
            dma((3,)),
        ],
        compiler_params=pltpu.CompilerParams(collective_id=0, has_side_effects=True),
    )(w_qkv, w_out, w_fc1, w_fc2, tokens, cotangent, ids)


def reduce_all(ndp, nt, sizes, partials, zin, bias_rows):
    shape = jax.ShapeDtypeStruct
    many = ndp * 2
    pq, po, p1, p2 = partials
    dma = pltpu.SemaphoreType.DMA
    shards_shape = (
        (pq.shape[0], pq.shape[1] // many, pq.shape[2]),
        (po.shape[0], po.shape[1] // many),
        (p1.shape[0] // many, p1.shape[1]),
        (p2.shape[0], p2.shape[1] // many),
    )
    stacks = [pltpu.VMEM((ndp,) + part, jnp.bfloat16) for part in shards_shape]
    rows = zin.shape[1] // nt
    bias_shape = bias_rows.shape
    return pl.pallas_call(
        functools.partial(reduce_kernel, ndp, nt, sizes),
        out_shape=tuple(shape(part, jnp.float32) for part in shards_shape)
        + (shape(zin.shape, zin.dtype), shape((2,) + bias_shape, jnp.float32)),
        in_specs=[ANY] * 4 + [VM] * 2,
        out_specs=[VM] * 6,
        scratch_shapes=stacks
        + stacks
        + stacks
        + [
            pltpu.VMEM((nt, zin.shape[0], rows, zin.shape[2]), zin.dtype),
            pltpu.VMEM(bias_shape, jnp.float32),
            pltpu.VMEM(bias_shape, jnp.float32),
            pltpu.VMEM((ndp,) + bias_shape, jnp.float32),
            pltpu.VMEM(bias_shape, jnp.float32),
            pltpu.VMEM((nt,) + bias_shape, jnp.float32),
            dma((4, ndp)),
            dma((4, ndp)),
            dma((4, ndp)),
            dma((4, ndp)),
            dma((4, ndp)),
            dma((nt,)),
            dma((nt,)),
            dma((nt,)),
            dma((nt,)),
            dma,
            dma,
            dma((ndp,)),
            dma((ndp,)),
            dma((nt,)),
            dma((nt,)),
        ],
        compiler_params=pltpu.CompilerParams(collective_id=1, has_side_effects=True),
    )(pq, po, p1, p2, zin, bias_rows)


def block(mesh, *args):
    seqs, rows, _ = args[0].shape
    heads = args[4].shape[2] // HD
    length = rows * mesh.shape["seq"]
    if mesh.shape["seq"] == 2 and seqs * heads * length * length * 4 <= 2**23:
        return whole_rows(mesh.shape["dp"], mesh.shape["tensor"], *args)
    return shards(*args)


def whole_rows(
    ndp,
    nt,
    block_input,
    cotangent,
    segments,
    positions,
    w_qkv,
    qkv_bias,
    w_out,
    w_fc1,
    fc1_bias,
    w_fc2,
    ln_gains,
    row_biases,
):
    seqs, rows, width = block_input.shape
    length = rows * 2
    heads = w_qkv.shape[2] // HD
    flat = heads * HD
    scale = HD ** (-0.5)
    f32, bf16 = jnp.float32, jnp.bfloat16
    sizes = (w_qkv.shape[1], w_out.shape[1], w_fc1.shape[0], w_fc2.shape[1])
    ids = jnp.stack([segments, positions], axis=1)
    wq, wo, w1, w2, xg, cg, idg = gather_all(
        ndp, sizes, w_qkv, w_out, w_fc1, w_fc2, block_input, cotangent, ids
    )
    x_all = xg.reshape(seqs, length, width)
    c_all = cg.reshape(seqs, length, width)
    seg = idg[:, :, 0].reshape(seqs, length)
    pos = idg[:, :, 1].reshape(seqs, length)
    start = lax.axis_index("seq") * rows

    def here(array):
        return lax.dynamic_slice_in_dim(array, start, rows, array.ndim - 2)

    first_all = layer_norm(x_all.astype(f32), ln_gains[0], row_biases[0])[0].astype(bf16)
    inputs_f = block_input.astype(f32)
    second_out, normed, inv_std = layer_norm(inputs_f, ln_gains[1], row_biases[1])
    second = second_out.astype(bf16)
    first = (normed * ln_gains[0] + row_biases[0]).astype(bf16)

    projected = (
        jnp.einsum("bxf,kfh->kbxh", first_all, wq, preferred_element_type=f32)
        + qkv_bias[:, None, None, :]
    )
    shape_heads = (seqs, length, heads, HD)
    cosine, sine = rotary_tables(pos)
    queries = rotate(projected[0].reshape(shape_heads), cosine, sine).astype(bf16)
    keys = rotate(projected[1].reshape(shape_heads), cosine, sine).astype(bf16)
    values = projected[2].reshape(shape_heads).astype(bf16)
    token = jnp.arange(length)
    allowed = (
        (seg[:, :, None] == seg[:, None, :]) & (token[None, None, :] <= token[None, :, None])
    )[:, None]
    scores = jnp.einsum("sqhd,skhd->shqk", queries, keys, preferred_element_type=f32) * scale
    row_max = jnp.max(jnp.where(allowed, scores, neg_big), axis=-1, keepdims=True)
    expo = jnp.where(allowed, jnp.exp(scores - row_max), 0.0)
    row_sum = jnp.sum(expo, axis=-1, keepdims=True)
    mixed = jnp.einsum("shqk,skhd->shqd", expo.astype(bf16), values, preferred_element_type=f32)
    context = (mixed / row_sum).transpose(0, 2, 1, 3).reshape(seqs, length, flat).astype(bf16)
    grad_context = jnp.einsum("sli,zi->slz", c_all, wo, preferred_element_type=f32).astype(bf16)
    grad_ctx_heads = grad_context.reshape(shape_heads)
    delta = jnp.sum(
        grad_ctx_heads.astype(f32) * context.reshape(shape_heads).astype(f32), axis=-1
    ).transpose(0, 2, 1)
    probs = expo / row_sum
    grad_p = jnp.einsum("sqhd,skhd->shqk", grad_ctx_heads, values, preferred_element_type=f32)
    grad_s = (probs * (grad_p - delta[..., None])).astype(bf16)
    grad_v = jnp.einsum(
        "shqk,sqhd->skhd", probs.astype(bf16), grad_ctx_heads, preferred_element_type=f32
    )
    grad_q = jnp.einsum("shqk,skhd->sqhd", grad_s, keys, preferred_element_type=f32) * scale
    grad_k = jnp.einsum("shqk,sqhd->skhd", grad_s, queries, preferred_element_type=f32) * scale
    grad_proj = jnp.stack(
        [
            here(unrotate(grad_q, cosine, sine).reshape(seqs, length, flat)),
            here(unrotate(grad_k, cosine, sine).reshape(seqs, length, flat)),
            here(grad_v.reshape(seqs, length, flat)),
        ]
    )
    context_here = here(context)
    grad_bias_qkv = jnp.sum(grad_proj, axis=(1, 2))
    grad_proj_in = grad_proj.astype(bf16)

    pre_act = jnp.einsum("vrk,kt->vrt", second, w1, preferred_element_type=f32) + fc1_bias
    activ, gelu_slope = gelu_pair(pre_act)
    hidden = activ.astype(bf16)
    branches = jnp.einsum("qhw,wj->qhj", context_here, wo, preferred_element_type=f32) + jnp.einsum(
        "qzg,gc->qzc", hidden, w2, preferred_element_type=f32
    )
    grad_f = cotangent.astype(f32)
    grad_pre = jnp.einsum("hvg,rg->hvr", cotangent, w2, preferred_element_type=f32) * gelu_slope
    grad_hidden = grad_pre.astype(bf16)
    grad_second = jnp.einsum("ikq,uq->iku", grad_hidden, w1, preferred_element_type=f32)
    grad_first = jnp.einsum("etbp,eop->tbo", grad_proj_in, wq, preferred_element_type=f32)
    partials = (
        jnp.einsum("ink,oint->okt", first, grad_proj_in, preferred_element_type=f32).astype(bf16),
        jnp.einsum("bxz,bxe->ze", context_here, cotangent, preferred_element_type=f32).astype(bf16),
        jnp.einsum("mxa,mxr->ar", second, grad_hidden, preferred_element_type=f32).astype(bf16),
        jnp.einsum("tzi,tzo->io", hidden, cotangent, preferred_element_type=f32).astype(bf16),
    )
    scaled = grad_first * ln_gains[0] + grad_second * ln_gains[1]
    hid = w_fc1.shape[1]
    wide = max(width, hid, qkv_bias.size)
    line = lambda v: jnp.pad(v.reshape(-1), (0, wide - v.size))
    bias_rows = jnp.stack(
        [
            line(jnp.sum(grad_pre, axis=(0, 1))),
            line(grad_bias_qkv),
            line(jnp.sum(grad_first * normed, axis=(0, 1))),
            line(jnp.sum(grad_second * normed, axis=(0, 1))),
            line(jnp.sum(grad_first, axis=(0, 1))),
            line(jnp.sum(grad_second, axis=(0, 1))),
            line(jnp.sum(grad_f, axis=(0, 1))),
            jnp.zeros((wide,), f32),
        ]
    )
    zin = jnp.stack([branches, scaled]).astype(bf16).reshape(2, seqs * rows, width)
    gq, go, g1, g2, zsum, bias = reduce_all(ndp, nt, sizes, partials, zin, bias_rows)
    zsum = zsum.astype(f32).reshape(2, seqs, rows, width)
    output = (inputs_f + zsum[0] + row_biases[2] + row_biases[3]).astype(bf16)
    centre = jnp.mean(zsum[1], axis=-1, keepdims=True)
    slope = jnp.mean(zsum[1] * normed, axis=-1, keepdims=True)
    grad_input = grad_f + inv_std * (zsum[1] - centre - normed * slope)
    total = bias[1, :, :width]
    grad_ct = bias[0, 6, :width]
    return (
        output,
        grad_input,
        gq,
        go,
        g1,
        g2,
        bias[0, 1, : qkv_bias.size].reshape(qkv_bias.shape),
        bias[0, 0, :hid],
        total[2:4],
        jnp.stack([total[4], total[5], grad_ct, grad_ct]),
    )


def solution(mesh):
    return jax.shard_map(
        functools.partial(block, mesh),
        mesh=mesh,
        in_specs=(
            P("dp", "seq", None),
            P("dp", "seq", None),
            P("dp", "seq"),
            P("dp", "seq"),
            P(None, ("dp", "seq"), "tensor"),
            P(None, "tensor"),
            P("tensor", ("dp", "seq")),
            P(("dp", "seq"), "tensor"),
            P("tensor"),
            P("tensor", ("dp", "seq")),
            P(),
            P(),
        ),
        out_specs=(
            P("dp", "seq", None),
            P("dp", "seq", None),
            P(None, ("dp", "seq"), "tensor"),
            P("tensor", ("dp", "seq")),
            P(("dp", "seq"), "tensor"),
            P("tensor", ("dp", "seq")),
            P(None, "tensor"),
            P("tensor"),
            P(),
            P(),
        ),
        check_vma=False,
    )
```

```python
import functools
import math

import jax
import jax.numpy as jnp
from jax import lax
from jax.experimental import pallas as pl
from jax.experimental.pallas import tpu as pltpu
from jax.sharding import PartitionSpec as P

HD = 64
ROT = 16


norm_eps = 1e-05
neg_big = -1e30
inv_root_two = 0.7071067811865476
inv_root_tau = 0.3989422804014327


def layer_norm(values, gain, shift):
    centred = values - jnp.mean(values, axis=-1, keepdims=True)
    inv_std = lax.rsqrt(jnp.mean(centred * centred, axis=-1, keepdims=True) + norm_eps)
    normed = centred * inv_std
    return (normed * gain + shift, normed, inv_std)


def norm_back(grad_out, normed, inv_std, gain):
    scaled = grad_out * gain
    centre = jnp.mean(scaled, axis=-1, keepdims=True)
    slope = jnp.mean(scaled * normed, axis=-1, keepdims=True)
    return inv_std * (scaled - centre - normed * slope)


def gelu_pair(pre_act):
    cumul = 0.5 * (1.0 + lax.erf(pre_act * inv_root_two))
    return (pre_act * cumul, cumul + pre_act * inv_root_tau * jnp.exp(-0.5 * pre_act * pre_act))


def rotary_tables(positions):
    half_rot = ROT // 2
    freqs = 10000.0 ** (-2.0 * jnp.arange(half_rot).astype(jnp.float32) / ROT)
    angles = positions.astype(jnp.float32)[..., None] * freqs
    cosine = jnp.cos(angles)
    sine = jnp.sin(angles)
    return (
        jnp.concatenate([cosine, cosine], -1)[..., None, :],
        jnp.concatenate([sine, sine], -1)[..., None, :],
    )


def rotate(tensor, cosine, sine):
    half_rot = ROT // 2
    head = tensor[..., :ROT]
    turned = jnp.concatenate([-head[..., half_rot:], head[..., :half_rot]], -1)
    return jnp.concatenate([head * cosine + turned * sine, tensor[..., ROT:]], -1)


def unrotate(grads, cosine, sine):
    half_rot = ROT // 2
    head = grads[..., :ROT]
    times_sine = head * sine
    back = jnp.concatenate([times_sine[..., half_rot:], -times_sine[..., :half_rot]], -1)
    return jnp.concatenate([head * cosine + back, grads[..., ROT:]], -1)


def gather_keys(keys_flat, values_in, segments):
    return (
        lax.all_gather(keys_flat, "seq", axis=1, tiled=True),
        lax.all_gather(values_in, "seq", axis=1, tiled=True),
        lax.all_gather(segments, "seq", axis=1, tiled=True),
    )


def pair_terms(
    query_blk,
    query_pos,
    query_seg,
    key_blk,
    value_blk,
    key_pos,
    key_seg,
    grad_blk,
    log_blk,
    delta_blk,
    scale,
):
    scores = (
        jnp.einsum("sqhd,skhd->shqk", query_blk, key_blk, preferred_element_type=jnp.float32)
        * scale
    )
    same_doc = query_seg[:, None, :, None] == key_seg[:, None, None, :]
    earlier = key_pos[None, None, None, :] <= query_pos[None, None, :, None]
    probs = jnp.where(same_doc & earlier, jnp.exp(scores - log_blk[..., None]), 0.0)
    grad_p = jnp.einsum("sqhd,skhd->shqk", grad_blk, value_blk, preferred_element_type=jnp.float32)
    grad_s = (probs * (grad_p - delta_blk[..., None])).astype(jnp.bfloat16)
    return (probs, grad_s)


def shards(
    block_input,
    cotangent,
    segments,
    positions,
    w_qkv,
    qkv_bias,
    w_out,
    w_fc1,
    fc1_bias,
    w_fc2,
    ln_gains,
    row_biases,
):
    seqs_here, rows_here, width = block_input.shape
    heads_here = w_qkv.shape[2] // HD
    flat_width = heads_here * HD
    scale = HD ** (-0.5)
    shape_heads = (seqs_here, rows_here, heads_here, HD)
    forward_weights = (
        lax.all_gather(w_qkv, ("dp", "seq"), axis=1, tiled=True),
        lax.all_gather(w_out, ("dp", "seq"), axis=1, tiled=True),
        lax.all_gather(w_fc1, ("dp", "seq"), axis=0, tiled=True),
        lax.all_gather(w_fc2, ("dp", "seq"), axis=1, tiled=True),
    )
    query_key_value_gathered, output_weight_gathered, up_weight_gathered, down_weight_gathered = (
        forward_weights
    )
    inputs_f = block_input.astype(jnp.float32)
    first_out, first_normed, first_inv = layer_norm(inputs_f, ln_gains[0], row_biases[0])
    second_out, second_normed, second_inv = layer_norm(inputs_f, ln_gains[1], row_biases[1])
    first_norm_input = first_out.astype(jnp.bfloat16)
    second_norm_input = second_out.astype(jnp.bfloat16)
    projected = (
        jnp.einsum(
            "bxf,kfh->kbxh",
            first_norm_input,
            query_key_value_gathered,
            preferred_element_type=jnp.float32,
        )
        + qkv_bias[:, None, None, :]
    )
    cosine, sine = rotary_tables(positions)
    queries = rotate(projected[0].reshape(shape_heads), cosine, sine).astype(jnp.bfloat16)
    keys_flat = (
        rotate(projected[1].reshape(shape_heads), cosine, sine)
        .astype(jnp.bfloat16)
        .reshape(seqs_here, rows_here, flat_width)
    )
    values_in = projected[2].astype(jnp.bfloat16)
    query_pos = lax.axis_index("seq") * rows_here + jnp.arange(rows_here)

    def block_scores(key_block, seg_block, key_start):
        count = key_block.shape[1]
        keys_heads = key_block.reshape(seqs_here, count, heads_here, HD)
        scores = (
            jnp.einsum("sqhd,skhd->shqk", queries, keys_heads, preferred_element_type=jnp.float32)
            * scale
        )
        key_pos = key_start + jnp.arange(count)
        same_doc = segments[:, None, :, None] == seg_block[:, None, None, :]
        earlier = key_pos[None, None, None, :] <= query_pos[None, None, :, None]
        return (scores, same_doc & earlier)

    start_state = (
        jnp.full((seqs_here, heads_here, rows_here), neg_big, jnp.float32),
        jnp.zeros((seqs_here, heads_here, rows_here), jnp.float32),
        jnp.zeros((seqs_here, heads_here, rows_here, HD), jnp.float32),
    )
    key_part = lax.all_gather(keys_flat, "seq", axis=1, tiled=True)
    value_part = lax.all_gather(values_in, "seq", axis=1, tiled=True)
    seg_part = lax.all_gather(segments, "seq", axis=1, tiled=True)
    count = key_part.shape[1]
    attend_block = math.gcd(count, 512)

    def step_block(block_idx, state):
        run_max, run_sum, accum = state
        offset = block_idx * attend_block
        key_block = lax.dynamic_slice_in_dim(key_part, offset, attend_block, 1)
        value_block = lax.dynamic_slice_in_dim(value_part, offset, attend_block, 1).reshape(
            seqs_here, attend_block, heads_here, HD
        )
        seg_block = lax.dynamic_slice_in_dim(seg_part, offset, attend_block, 1)
        scores, allowed = block_scores(key_block, seg_block, offset)
        new_max = jnp.maximum(run_max, jnp.max(jnp.where(allowed, scores, neg_big), axis=-1))
        factor = jnp.exp(run_max - new_max)
        expo = jnp.where(allowed, jnp.exp(scores - new_max[..., None]), 0.0)
        new_sum = run_sum * factor + jnp.sum(expo, axis=-1)
        update = jnp.einsum(
            "shqk,skhd->shqd",
            expo.astype(jnp.bfloat16),
            value_block,
            preferred_element_type=jnp.float32,
        )
        return (new_max, new_sum, accum * factor[..., None] + update)

    run_max, run_sum, accum = lax.fori_loop(0, count // attend_block, step_block, start_state)
    log_sum = run_max + jnp.log(run_sum)
    attention_context = (
        (accum / run_sum[..., None])
        .transpose(0, 2, 1, 3)
        .reshape(seqs_here, rows_here, flat_width)
        .astype(jnp.bfloat16)
    )
    pre_act = (
        jnp.einsum(
            "vrk,kt->vrt", second_norm_input, up_weight_gathered, preferred_element_type=jnp.float32
        )
        + fc1_bias
    )
    activ, gelu_slope = gelu_pair(pre_act)
    hidden_activation = activ.astype(jnp.bfloat16)
    partial_output_sum = jnp.einsum(
        "qhw,wj->qhj", attention_context, output_weight_gathered, preferred_element_type=jnp.float32
    )
    partial_output_sum = partial_output_sum + jnp.einsum(
        "qzg,gc->qzc", hidden_activation, down_weight_gathered, preferred_element_type=jnp.float32
    )
    branches = lax.psum(partial_output_sum.astype(jnp.bfloat16), "tensor").astype(jnp.float32)
    output = (inputs_f + branches + row_biases[2] + row_biases[3]).astype(jnp.bfloat16)
    query_key_value_backward, output_weight_backward, up_weight_backward, down_weight_backward = (
        lax.all_gather(w_qkv, ("dp", "seq"), axis=1, tiled=True),
        lax.all_gather(w_out, ("dp", "seq"), axis=1, tiled=True),
        lax.all_gather(w_fc1, ("dp", "seq"), axis=0, tiled=True),
        lax.all_gather(w_fc2, ("dp", "seq"), axis=1, tiled=True),
    )
    grad_f = cotangent.astype(jnp.float32)
    gradient_output_weight = jnp.einsum(
        "bxz,bxe->ze", attention_context, cotangent, preferred_element_type=jnp.float32
    )
    grad_context = jnp.einsum(
        "zpi,xi->zpx", cotangent, output_weight_backward, preferred_element_type=jnp.float32
    ).astype(jnp.bfloat16)
    gradient_down_weight = jnp.einsum(
        "tzi,tzo->io", hidden_activation, cotangent, preferred_element_type=jnp.float32
    )
    grad_pre = (
        jnp.einsum(
            "hvg,rg->hvr", cotangent, down_weight_backward, preferred_element_type=jnp.float32
        )
        * gelu_slope
    )
    gradient_hidden_input = grad_pre.astype(jnp.bfloat16)
    grad_fc1_w = jnp.einsum(
        "mxa,mxr->ar", second_norm_input, gradient_hidden_input, preferred_element_type=jnp.float32
    )
    grad_second = jnp.einsum(
        "ikq,uq->iku", gradient_hidden_input, up_weight_backward, preferred_element_type=jnp.float32
    )
    grad_ctx_heads = grad_context.reshape(shape_heads)
    delta = jnp.sum(
        grad_ctx_heads.astype(jnp.float32)
        * attention_context.reshape(shape_heads).astype(jnp.float32),
        axis=-1,
    ).transpose(0, 2, 1)
    key_all, value_all, seg_all = gather_keys(keys_flat, values_in, segments)
    total_len = key_all.shape[1]
    block = math.gcd(total_len, 512)

    def key_slices(offset):
        key_block = lax.dynamic_slice_in_dim(key_all, offset, block, 1).reshape(
            seqs_here, block, heads_here, HD
        )
        value_block = lax.dynamic_slice_in_dim(value_all, offset, block, 1).reshape(
            seqs_here, block, heads_here, HD
        )
        seg_block = lax.dynamic_slice_in_dim(seg_all, offset, block, 1)
        return (key_block, value_block, seg_block)

    def back_block(block_idx, state):
        grad_q, grad_key_all, grad_value_all = state
        offset = block_idx * block
        key_block, value_block, seg_block = key_slices(offset)
        probs, grad_s = pair_terms(
            queries,
            query_pos,
            segments,
            key_block,
            value_block,
            offset + jnp.arange(block),
            seg_block,
            grad_ctx_heads,
            log_sum,
            delta,
            scale,
        )
        grad_v = jnp.einsum(
            "shqk,sqhd->skhd",
            probs.astype(jnp.bfloat16),
            grad_ctx_heads,
            preferred_element_type=jnp.float32,
        )
        grad_q = (
            grad_q
            + jnp.einsum("shqk,skhd->sqhd", grad_s, key_block, preferred_element_type=jnp.float32)
            * scale
        )
        grad_k = (
            jnp.einsum("shqk,sqhd->skhd", grad_s, queries, preferred_element_type=jnp.float32)
            * scale
        )
        grad_key_all = lax.dynamic_update_slice_in_dim(
            grad_key_all, grad_k.reshape(seqs_here, block, flat_width), offset, 1
        )
        grad_value_all = lax.dynamic_update_slice_in_dim(
            grad_value_all, grad_v.reshape(seqs_here, block, flat_width), offset, 1
        )
        return (grad_q, grad_key_all, grad_value_all)

    back_start = (
        jnp.zeros(shape_heads, jnp.float32),
        jnp.zeros((seqs_here, total_len, flat_width), jnp.float32),
        jnp.zeros((seqs_here, total_len, flat_width), jnp.float32),
    )
    grad_q, grad_key_all, grad_value_all = lax.fori_loop(
        0, total_len // block, back_block, back_start
    )
    grad_key_here, grad_value_here = (
        lax.psum_scatter(
            grad_key_all.astype(jnp.bfloat16), "seq", scatter_dimension=1, tiled=True
        ).astype(jnp.float32),
        lax.psum_scatter(
            grad_value_all.astype(jnp.bfloat16), "seq", scatter_dimension=1, tiled=True
        ).astype(jnp.float32),
    )
    grad_proj = jnp.stack(
        [
            unrotate(grad_q, cosine, sine).reshape(seqs_here, rows_here, flat_width),
            unrotate(grad_key_here.reshape(shape_heads), cosine, sine).reshape(
                seqs_here, rows_here, flat_width
            ),
            grad_value_here,
        ]
    )
    grad_bias_qkv = jnp.sum(grad_proj, axis=(1, 2))
    gradient_projection_input = grad_proj.astype(jnp.bfloat16)
    grad_qkv_w = jnp.einsum(
        "ink,oint->okt",
        first_norm_input,
        gradient_projection_input,
        preferred_element_type=jnp.float32,
    )
    grad_first = jnp.einsum(
        "etbp,eop->tbo",
        gradient_projection_input,
        query_key_value_backward,
        preferred_element_type=jnp.float32,
    )
    grad_first, grad_second = (
        lax.psum(grad_first.astype(jnp.bfloat16), "tensor").astype(jnp.float32),
        lax.psum(grad_second.astype(jnp.bfloat16), "tensor").astype(jnp.float32),
    )
    grad_input = (
        grad_f
        + norm_back(grad_first, first_normed, first_inv, ln_gains[0])
        + norm_back(grad_second, second_normed, second_inv, ln_gains[1])
    )
    gain_terms = jnp.stack(
        [
            jnp.sum(grad_first * first_normed, axis=(0, 1)),
            jnp.sum(grad_second * second_normed, axis=(0, 1)),
        ]
    )
    row_terms = jnp.stack(
        [
            jnp.sum(grad_first, axis=(0, 1)),
            jnp.sum(grad_second, axis=(0, 1)),
            jnp.sum(grad_f, axis=(0, 1)),
            jnp.sum(grad_f, axis=(0, 1)),
        ]
    )
    bias_sums = lax.psum(
        (grad_bias_qkv, jnp.sum(grad_pre, axis=(0, 1)), gain_terms, row_terms), ("dp", "seq")
    )
    weight_sums = (
        lax.psum_scatter(grad_qkv_w, ("dp", "seq"), scatter_dimension=1, tiled=True),
        lax.psum_scatter(gradient_output_weight, ("dp", "seq"), scatter_dimension=1, tiled=True),
        lax.psum_scatter(grad_fc1_w, ("dp", "seq"), scatter_dimension=0, tiled=True),
        lax.psum_scatter(gradient_down_weight, ("dp", "seq"), scatter_dimension=1, tiled=True),
    )
    return (
        output,
        grad_input,
        weight_sums[0],
        weight_sums[1],
        weight_sums[2],
        weight_sums[3],
        bias_sums[0],
        bias_sums[1],
        bias_sums[2],
        bias_sums[3],
    )


MESH = pl.DeviceIdType.MESH
ANY = pl.BlockSpec(memory_space=pl.ANY)
VM = pl.BlockSpec(memory_space=pltpu.VMEM)


def remote(src, dst, send, recv, where):
    return pltpu.make_async_remote_copy(
        src_ref=src, dst_ref=dst, send_sem=send, recv_sem=recv, device_id=where, device_id_type=MESH
    )


def slots(n):
    return ((0, False), (1, True), (2, True), (3, False), (4, False), (5, True))[:n]


def pieces(refs, index, sizes):
    spans = [pl.ds(pl.multiple_of(index * n, n), n) for n in sizes]
    return (
        refs[0].at[0, spans[0], :],
        refs[0].at[1, spans[0], :],
        refs[0].at[2, spans[0], :],
        refs[1].at[:, spans[1]],
        refs[2].at[spans[2], :],
        refs[3].at[:, spans[3]],
    )


def plane_peers(d):
    return d + 1 - 2 * lax.rem(d, 2), lax.rem(d + 2, 4), 3 - d


def gather_kernel(sizes, *refs):
    (wq, wo, w1, w2, x, c, sp, gq, go, g1, g2, gx, gc, gsp) = refs[:14]
    send, recv, send2, recv2, local, psend, precv, plocal = refs[14:]
    nseq = 2
    d, s = lax.axis_index("dp"), lax.axis_index("seq")
    other = 1 - s
    near_x, near_y, corner = plane_peers(d)
    shards_in = (wq.at[0], wq.at[1], wq.at[2], wo, w1, w2)
    full = (gq, go, g1, g2)
    pairs = ((x, gx), (c, gc), (sp, gsp))

    barrier = pltpu.get_barrier_semaphore()
    for peer in (near_x, near_y):
        pl.semaphore_signal(barrier, inc=1, device_id={"dp": peer}, device_id_type=MESH)
    pl.semaphore_signal(barrier, inc=1, device_id={"seq": other}, device_id_type=MESH)
    pl.semaphore_wait(barrier, 3)

    mine = pieces(full, d * nseq + s, sizes)
    from_x = pieces(full, near_x * nseq + s, sizes)
    from_y = pieces(full, near_y * nseq + s, sizes)
    from_corner = pieces(full, corner * nseq + s, sizes)
    hops = {}
    copies = []
    locals_ = []
    for a, x_first in slots(6):
        order = ((0, near_x), (1, near_y)) if x_first else ((1, near_y), (0, near_x))
        for way, peer in order:
            copy = remote(shards_in[a], mine[a], send.at[a, way], recv.at[a, way], {"dp": peer})
            copy.start()
            hops[a, way] = copy
    for j, (src, dst) in enumerate(pairs):
        copy = remote(src, dst.at[:, s], psend.at[j], precv.at[j], {"seq": other})
        copy.start()
        copies.append(copy)
        copy = pltpu.make_async_copy(src, dst.at[:, s], plocal.at[j])
        copy.start()
        locals_.append(copy)
    for a, _ in slots(6):
        copy = remote(shards_in[a], mine[a], send2.at[a, 0], recv2.at[a, 0], {"seq": other})
        copy.start()
        copies.append(copy)
        copy = pltpu.make_async_copy(shards_in[a], mine[a], local.at[a])
        copy.start()
        locals_.append(copy)

    def across(a, slot, view):
        copy = remote(view, view, send2.at[a, slot], recv2.at[a, slot], {"seq": other})
        copy.start()
        copies.append(copy)

    last = {}
    for a, x_first in slots(6):
        for way in (0, 1) if x_first else (1, 0):
            hops[a, way].wait_recv()
            view = (from_x, from_y)[way][a]
            if x_first == (way == 0):
                peer = near_y if x_first else near_x
                copy = remote(view, view, send.at[a, 2], recv.at[a, 2], {"dp": peer})
                copy.start()
                last[a] = copy
            across(a, 1 + way, view)
    for a, _ in slots(6):
        last[a].wait_recv()
        across(a, 3, from_corner[a])
    for copy in locals_:
        copy.wait()
    for copy in hops.values():
        copy.wait_send()
    for copy in last.values():
        copy.wait_send()
    for copy in copies:
        copy.wait()


def across_tokens(left, right):
    return lax.dot_general(
        left, right, (((0,), (0,)), ((), ())), preferred_element_type=jnp.float32
    )


def reduce_kernel(nt, sizes, *refs):
    (first, gproj, ctx, cot, second, ghid, hid, zbr, zgr, tokens, rowb, bin_) = refs[:12]
    (oq, oo, o1, o2, yout, gout, bout) = refs[12:19]
    give, own, got1, got2, got3 = (refs[19 + 6 * i : 25 + 6 * i] for i in range(5))
    zgot, bpair, bsum, bgot2, bsum2, bgot3 = refs[49:55]
    (s1, r1, s2, r2, zs, zr, as_, ar, b1s, b1r, b2s, b2r, b3s, b3r) = refs[55:]
    nseq = 2
    ndp = 4
    d, s, t = lax.axis_index("dp"), lax.axis_index("seq"), lax.axis_index("tensor")
    other = 1 - s
    near_x, near_y, corner = plane_peers(d)
    rows = zbr.shape[0] // nt
    outs = (oq.at[0], oq.at[1], oq.at[2], oo, o1, o2)

    barrier = pltpu.get_barrier_semaphore()
    for peer in (near_x, near_y, corner):
        pl.semaphore_signal(barrier, inc=1, device_id={"dp": peer}, device_id_type=MESH)
    for k in range(1, nt):
        pl.semaphore_signal(
            barrier, inc=1, device_id={"tensor": lax.rem(t + k, nt)}, device_id_type=MESH
        )
    pl.semaphore_signal(barrier, inc=1, device_id={"seq": other}, device_id_type=MESH)
    pl.semaphore_wait(barrier, ndp + nt - 1)

    def band(index):
        return pl.ds(pl.multiple_of(index * rows, rows), rows)

    zsends = {}
    for j, src in enumerate((zbr, zgr)):
        for k in range(1, nt):
            peer = lax.rem(t + k, nt)
            copy = remote(
                src.at[band(peer), :], zgot.at[j, k], zs.at[j, k], zr.at[j, k], {"tensor": peer}
            )
            copy.start()
            zsends[j, k] = copy
    bpair_copy = remote(bin_, bpair, b1s, b1r, {"seq": other})
    bpair_copy.start()

    def product(a, index):
        span = lambda n: pl.ds(pl.multiple_of(index * n, n), n)
        if a < 3:
            return across_tokens(first[:, span(sizes[0])], gproj[a])
        if a == 3:
            return across_tokens(ctx[...], cot[:, span(sizes[1])])
        if a == 4:
            return across_tokens(second[:, span(sizes[2])], ghid[...])
        return across_tokens(hid[...], cot[:, span(sizes[3])])

    places = (d, near_x, near_y, corner)
    big_first = ((5, True), (4, False), (2, True), (0, False), (1, True), (3, False))
    pair = {}
    hop1 = {}
    hop2 = {}

    def make(where):
        for a, _ in big_first:
            give[a][where] = product(a, places[where] * nseq + other).astype(jnp.bfloat16)
            copy = remote(
                give[a].at[where], got1[a].at[where], s1.at[a, where], r1.at[a, where], {"seq": other}
            )
            copy.start()
            pair[a, where] = copy
        for a, _ in big_first:
            own[a][where] = product(a, places[where] * nseq + s).astype(jnp.bfloat16)

    def merge(a, where):
        pair[a, where].wait_recv()
        own[a][where] = (
            own[a][where].astype(jnp.float32) + got1[a][where].astype(jnp.float32)
        ).astype(jnp.bfloat16)

    def hop(a, x_first, where, slot):
        peer = near_x if x_first else near_y
        copy = remote(
            own[a].at[where], got2[a].at[slot], s2.at[a, slot], r2.at[a, slot], {"dp": peer}
        )
        copy.start()
        hop1[a, slot] = copy

    make(3)
    make(1)
    for a, x_first in big_first:
        merge(a, 3)
        hop(a, x_first, 3, 1)
    make(2)
    for a, x_first in big_first:
        if x_first:
            merge(a, 1)
            hop(a, x_first, 1, 0)
    for a, x_first in big_first:
        if not x_first:
            merge(a, 2)
            hop(a, x_first, 2, 0)
    make(0)
    for a, x_first in big_first:
        merge(a, 2 if x_first else 1)
        merge(a, 0)

    bpair_copy.wait()
    bsum[...] = bin_[...] + bpair[...]
    bsends = []
    for k, peer in ((1, near_x), (2, near_y), (3, corner)):
        copy = remote(bsum, bgot2.at[d], b2s.at[k], b2r.at[k], {"dp": peer})
        copy.start()
        bsends.append(copy)

    for a, x_first in big_first:
        hop1[a, 1].wait_recv()
        mid = 2 if x_first else 1
        own[a][mid] = (
            own[a][mid].astype(jnp.float32) + got2[a][1].astype(jnp.float32)
        ).astype(jnp.bfloat16)
        copy = remote(
            own[a].at[mid],
            got3[a],
            s2.at[a, 2],
            r2.at[a, 2],
            {"dp": near_y if x_first else near_x},
        )
        copy.start()
        hop2[a] = copy
    for a, _ in big_first:
        hop1[a, 0].wait_recv()
    zfull = []
    for j, src in enumerate((zbr, zgr)):
        total = src[band(t), :].astype(jnp.float32)
        for k in range(1, nt):
            zsends[j, k].wait_recv()
            total = total + zgot[j, k].astype(jnp.float32)
        zfull.append(total)
    inputs = tokens[band(t), :].astype(jnp.float32)
    _, normed, inv_std = layer_norm(inputs, 1.0, 0.0)
    yout[band(t), :] = (inputs + zfull[0] + rowb[2:3, :] + rowb[3:4, :]).astype(yout.dtype)
    gout[band(t), :] = norm_back(zfull[1], normed, inv_std, 1.0).astype(gout.dtype)
    asends = []
    for j, dst in enumerate((yout, gout)):
        for k in range(1, nt):
            copy = remote(
                dst.at[band(t), :],
                dst.at[band(t), :],
                as_.at[j, k],
                ar.at[j, k],
                {"tensor": lax.rem(t + k, nt)},
            )
            copy.start()
            asends.append(copy)
    for copy in bsends:
        copy.wait()
    bgot2[d] = bsum[...]
    plane = bgot2[0]
    for k in range(1, ndp):
        plane = plane + bgot2[k]
    bsum2[...] = plane
    bsends = []
    for k in range(1, nt):
        copy = remote(bsum2, bgot3.at[t], b3s.at[k], b3r.at[k], {"tensor": lax.rem(t + k, nt)})
        copy.start()
        bsends.append(copy)

    for a, x_first in big_first:
        hop2[a].wait_recv()
        outs[a][...] = (
            own[a][0].astype(jnp.float32)
            + got2[a][0].astype(jnp.float32)
            + got3[a][...].astype(jnp.float32)
        )
    for copy in bsends:
        copy.wait()
    bgot3[t] = bsum2[...]
    whole = bgot3[0]
    for k in range(1, nt):
        whole = whole + bgot3[k]
    bout[0] = bsum2[...]
    bout[1] = whole
    for copy in asends:
        copy.wait()
    for group in (zsends, pair, hop1, hop2):
        for copy in group.values():
            copy.wait_send()


def gather_all(ndp, sizes, w_qkv, w_out, w_fc1, w_fc2, tokens, cotangent, ids):
    shape = jax.ShapeDtypeStruct
    many = ndp * 2
    seqs, rows, width = tokens.shape
    dma = pltpu.SemaphoreType.DMA
    return pl.pallas_call(
        functools.partial(gather_kernel, sizes),
        out_shape=(
            shape((w_qkv.shape[0], w_qkv.shape[1] * many, w_qkv.shape[2]), w_qkv.dtype),
            shape((w_out.shape[0], w_out.shape[1] * many), w_out.dtype),
            shape((w_fc1.shape[0] * many, w_fc1.shape[1]), w_fc1.dtype),
            shape((w_fc2.shape[0], w_fc2.shape[1] * many), w_fc2.dtype),
            shape((seqs, 2, rows, width), tokens.dtype),
            shape((seqs, 2, rows, width), cotangent.dtype),
            shape((ids.shape[0], 2) + ids.shape[1:], ids.dtype),
        ),
        in_specs=[VM] * 7,
        out_specs=[ANY] * 7,
        scratch_shapes=[
            dma((6, 3)),
            dma((6, 3)),
            dma((6, 4)),
            dma((6, 4)),
            dma((6,)),
            dma((3,)),
            dma((3,)),
            dma((3,)),
        ],
        compiler_params=pltpu.CompilerParams(collective_id=0, has_side_effects=True),
    )(w_qkv, w_out, w_fc1, w_fc2, tokens, cotangent, ids)


def reduce_all(nt, sizes, operands, bias_rows):
    shape = jax.ShapeDtypeStruct
    first, gproj, ctx, cot, second, ghid, hid, zbr = operands[:8]
    dma = pltpu.SemaphoreType.DMA
    parts = ((sizes[0], gproj.shape[2]),) * 3 + (
        (ctx.shape[1], sizes[1]),
        (sizes[2], ghid.shape[1]),
        (hid.shape[1], sizes[3]),
    )
    stack = lambda n: [pltpu.VMEM((n,) + part, jnp.bfloat16) for part in parts]
    rows = zbr.shape[0] // nt
    bias_shape = bias_rows.shape
    return pl.pallas_call(
        functools.partial(reduce_kernel, nt, sizes),
        out_shape=(
            shape((3,) + parts[0], jnp.float32),
            shape(parts[3], jnp.float32),
            shape(parts[4], jnp.float32),
            shape(parts[5], jnp.float32),
            shape(zbr.shape, jnp.bfloat16),
            shape(zbr.shape, jnp.bfloat16),
            shape((2,) + bias_shape, jnp.float32),
        ),
        in_specs=[VM] * 12,
        out_specs=[VM] * 7,
        scratch_shapes=stack(4)
        + stack(4)
        + stack(4)
        + stack(2)
        + [pltpu.VMEM(part, jnp.bfloat16) for part in parts]
        + [
            pltpu.VMEM((2, nt, rows, zbr.shape[1]), jnp.bfloat16),
            pltpu.VMEM(bias_shape, jnp.float32),
            pltpu.VMEM(bias_shape, jnp.float32),
            pltpu.VMEM((4,) + bias_shape, jnp.float32),
            pltpu.VMEM(bias_shape, jnp.float32),
            pltpu.VMEM((nt,) + bias_shape, jnp.float32),
            dma((6, 4)),
            dma((6, 4)),
            dma((6, 3)),
            dma((6, 3)),
            dma((2, nt)),
            dma((2, nt)),
            dma((2, nt)),
            dma((2, nt)),
            dma,
            dma,
            dma((4,)),
            dma((4,)),
            dma((nt,)),
            dma((nt,)),
        ],
        compiler_params=pltpu.CompilerParams(collective_id=1, has_side_effects=True),
    )(*operands, bias_rows)


def block(mesh, *args):
    seqs, rows, _ = args[0].shape
    heads = args[4].shape[2] // HD
    length = rows * mesh.shape["seq"]
    if mesh.shape["seq"] == 2 and mesh.shape["dp"] == 4 and seqs * heads * length * length * 4 <= 2**23:
        return whole_rows(mesh.shape["dp"], mesh.shape["tensor"], *args)
    return shards(*args)


def whole_rows(
    ndp,
    nt,
    block_input,
    cotangent,
    segments,
    positions,
    w_qkv,
    qkv_bias,
    w_out,
    w_fc1,
    fc1_bias,
    w_fc2,
    ln_gains,
    row_biases,
):
    seqs, rows, width = block_input.shape
    length = rows * 2
    heads = w_qkv.shape[2] // HD
    flat = heads * HD
    scale = HD ** (-0.5)
    f32, bf16 = jnp.float32, jnp.bfloat16
    sizes = (w_qkv.shape[1], w_out.shape[1], w_fc1.shape[0], w_fc2.shape[1])
    ids = jnp.stack([segments, positions], axis=1)
    wq, wo, w1, w2, xg, cg, idg = gather_all(
        ndp, sizes, w_qkv, w_out, w_fc1, w_fc2, block_input, cotangent, ids
    )
    x_all = xg.reshape(seqs, length, width)
    c_all = cg.reshape(seqs, length, width)
    seg = idg[:, :, 0].reshape(seqs, length)
    pos = idg[:, :, 1].reshape(seqs, length)
    start = lax.axis_index("seq") * rows

    def here(array):
        return lax.dynamic_slice_in_dim(array, start, rows, array.ndim - 2)

    first_all = layer_norm(x_all.astype(f32), ln_gains[0], row_biases[0])[0].astype(bf16)
    inputs_f = block_input.astype(f32)
    second_out, normed, inv_std = layer_norm(inputs_f, ln_gains[1], row_biases[1])
    second = second_out.astype(bf16)
    first = (normed * ln_gains[0] + row_biases[0]).astype(bf16)

    projected = (
        jnp.einsum("bxf,kfh->kbxh", first_all, wq, preferred_element_type=f32)
        + qkv_bias[:, None, None, :]
    )
    shape_heads = (seqs, length, heads, HD)
    cosine, sine = rotary_tables(pos)
    queries = rotate(projected[0].reshape(shape_heads), cosine, sine).astype(bf16)
    keys = rotate(projected[1].reshape(shape_heads), cosine, sine).astype(bf16)
    values = projected[2].reshape(shape_heads).astype(bf16)
    token = jnp.arange(length)
    allowed = (
        (seg[:, :, None] == seg[:, None, :]) & (token[None, None, :] <= token[None, :, None])
    )[:, None]
    scores = jnp.einsum("sqhd,skhd->shqk", queries, keys, preferred_element_type=f32) * scale
    row_max = jnp.max(jnp.where(allowed, scores, neg_big), axis=-1, keepdims=True)
    expo = jnp.where(allowed, jnp.exp(scores - row_max), 0.0)
    row_sum = jnp.sum(expo, axis=-1, keepdims=True)
    mixed = jnp.einsum("shqk,skhd->shqd", expo.astype(bf16), values, preferred_element_type=f32)
    context = (mixed / row_sum).transpose(0, 2, 1, 3).reshape(seqs, length, flat).astype(bf16)
    grad_context = jnp.einsum("sli,zi->slz", c_all, wo, preferred_element_type=f32).astype(bf16)
    grad_ctx_heads = grad_context.reshape(shape_heads)
    delta = jnp.sum(
        grad_ctx_heads.astype(f32) * context.reshape(shape_heads).astype(f32), axis=-1
    ).transpose(0, 2, 1)
    probs = expo / row_sum
    grad_p = jnp.einsum("sqhd,skhd->shqk", grad_ctx_heads, values, preferred_element_type=f32)
    grad_s = (probs * (grad_p - delta[..., None])).astype(bf16)
    grad_v = jnp.einsum(
        "shqk,sqhd->skhd", probs.astype(bf16), grad_ctx_heads, preferred_element_type=f32
    )
    grad_q = jnp.einsum("shqk,skhd->sqhd", grad_s, keys, preferred_element_type=f32) * scale
    grad_k = jnp.einsum("shqk,sqhd->skhd", grad_s, queries, preferred_element_type=f32) * scale
    grad_proj = jnp.stack(
        [
            here(unrotate(grad_q, cosine, sine).reshape(seqs, length, flat)),
            here(unrotate(grad_k, cosine, sine).reshape(seqs, length, flat)),
            here(grad_v.reshape(seqs, length, flat)),
        ]
    )
    context_here = here(context)
    grad_bias_qkv = jnp.sum(grad_proj, axis=(1, 2))
    grad_proj_in = grad_proj.astype(bf16)

    pre_act = jnp.einsum("vrk,kt->vrt", second, w1, preferred_element_type=f32) + fc1_bias
    activ, gelu_slope = gelu_pair(pre_act)
    hidden = activ.astype(bf16)
    branches = jnp.einsum("qhw,wj->qhj", context_here, wo, preferred_element_type=f32) + jnp.einsum(
        "qzg,gc->qzc", hidden, w2, preferred_element_type=f32
    )
    grad_f = cotangent.astype(f32)
    grad_pre = jnp.einsum("hvg,rg->hvr", cotangent, w2, preferred_element_type=f32) * gelu_slope
    grad_hidden = grad_pre.astype(bf16)
    grad_second = jnp.einsum("ikq,uq->iku", grad_hidden, w1, preferred_element_type=f32)
    grad_first = jnp.einsum("etbp,eop->tbo", grad_proj_in, wq, preferred_element_type=f32)
    scaled = grad_first * ln_gains[0] + grad_second * ln_gains[1]
    hid = w_fc1.shape[1]
    wide = max(width, hid, qkv_bias.size)
    line = lambda v: jnp.pad(v.reshape(-1), (0, wide - v.size))
    bias_rows = jnp.stack(
        [
            line(jnp.sum(grad_pre, axis=(0, 1))),
            line(grad_bias_qkv),
            line(jnp.sum(grad_first * normed, axis=(0, 1))),
            line(jnp.sum(grad_second * normed, axis=(0, 1))),
            line(jnp.sum(grad_first, axis=(0, 1))),
            line(jnp.sum(grad_second, axis=(0, 1))),
            line(jnp.sum(grad_f, axis=(0, 1))),
            jnp.zeros((wide,), f32),
        ]
    )
    tall = lambda v: v.reshape(seqs * rows, -1).astype(bf16)
    operands = (
        tall(first),
        grad_proj_in.reshape(3, seqs * rows, flat),
        tall(context_here),
        tall(cotangent),
        tall(second),
        tall(grad_hidden),
        tall(hidden),
        tall(branches),
        tall(scaled),
        tall(block_input),
        row_biases,
    )
    gq, go, g1, g2, output, grad_norm, bias = reduce_all(nt, sizes, operands, bias_rows)
    output = output.reshape(seqs, rows, width)
    grad_input = grad_f + grad_norm.reshape(seqs, rows, width).astype(f32)
    total = bias[1, :, :width]
    grad_ct = bias[0, 6, :width]
    return (
        output,
        grad_input,
        gq,
        go,
        g1,
        g2,
        bias[0, 1, : qkv_bias.size].reshape(qkv_bias.shape),
        bias[0, 0, :hid],
        total[2:4],
        jnp.stack([total[4], total[5], grad_ct, grad_ct]),
    )


def solution(mesh):
    return jax.shard_map(
        functools.partial(block, mesh),
        mesh=mesh,
        in_specs=(
            P("dp", "seq", None),
            P("dp", "seq", None),
            P("dp", "seq"),
            P("dp", "seq"),
            P(None, ("dp", "seq"), "tensor"),
            P(None, "tensor"),
            P("tensor", ("dp", "seq")),
            P(("dp", "seq"), "tensor"),
            P("tensor"),
            P("tensor", ("dp", "seq")),
            P(),
            P(),
        ),
        out_specs=(
            P("dp", "seq", None),
            P("dp", "seq", None),
            P(None, ("dp", "seq"), "tensor"),
            P("tensor", ("dp", "seq")),
            P(("dp", "seq"), "tensor"),
            P("tensor", ("dp", "seq")),
            P(None, "tensor"),
            P("tensor"),
            P(),
            P(),
        ),
        check_vma=False,
    )
```
